32 devices in a mesh: grp: 4 (over z), head: 8 (over y, x, core).
Axes of the slice: x: 2, y: 2, z: 4, core: 2. Of those that a mesh axis runs over, the one named last changes fastest.
Arguments:
- inputs: bfloat16 [4, 64, 4096], P(None, 'grp', 'head'), parts along dimension 1, may hold values from -6 to 6
- gains: float32 [2, 4096], replicated, may hold values from 0.5 to 1.5
- decays: float32 [2, 32], P(None, 'head'), may hold values from 0.7 to 0.999
- w_qkv: bfloat16 [2, 4096, 3, 32, 128], P(None, None, None, 'head'), may hold values from -0.09375 to 0.09375
- w_out: bfloat16 [2, 32, 128, 4096], P(None, 'head'), may hold values from -0.125 to 0.125
- s_state: float32 [2, 64, 32, 128, 128], P(None, 'grp', 'head'), parts along dimension 1, may hold values from -0.5 to 0.5
- r_state: float32 [2, 64, 32, 128, 128], P(None, 'grp', 'head'), parts along dimension 1, as said below
Outputs:
- stream_out: float32 [4, 64, 4096], P(None, 'grp', 'head'), parts along dimension 1
- s_final: float32 [2, 64, 32, 128, 128], P(None, 'grp', 'head'), parts along dimension 1
- r_final: float32 [2, 64, 32, 128, 128], P(None, 'grp', 'head'), parts along dimension 1
The draws below stay inside these ranges and needn't reach their ends.
There are 4 independent parts, one for each index of `grp`. The reference program is written for one: setup_inputs(seed, part) draws one part's arguments, and reference() takes and returns one part's arrays. A program takes and returns all parts, laid end to end along the dimension named above; an argument that names none is the same for every part. Nothing has to cross between parts.
Inputs may be any that keep to these rules, and one draw needn't show every extreme that they name: `r_state`: each matrix is symmetric positive definite with eigenvalues of 0.5 or more and of order one.
All inputs are finite; a program needn't handle non-finite values.
Results may differ from the reference program's by a relative error of at most 0.02.
Values may be sent and summed in bfloat16 or wider, within the bound.
A program may use at most 192 MiB of HBM per device.

```python
import math
import jax
import jax.numpy as jnp
from jax import lax

D = 4096
H = 32
HD = 128
B = 16
TOKS = 4
LAYERS = 2


def draw_r_state(key, part):
    factor = jax.random.normal(key, (LAYERS, B, H, HD, HD), jnp.float32)
    product = jnp.einsum('lbhij,lbhkj->lbhik', factor, factor, precision=lax.Precision.HIGHEST)
    return 0.5 * jnp.eye(HD, dtype=jnp.float32) + product / HD


def spiked(values, key, source, target, parts, factor):
    owner, partner = [(jnp.arange(values.shape[dim]) // (values.shape[dim] // parts)).reshape([-1 if axis == dim else 1 for axis in range(values.ndim)]) for dim in (source, target)]
    chosen = jax.random.permutation(key, parts)[partner]
    strong = (owner == chosen) | (owner == (partner + parts // 2) % parts)
    return jnp.where(strong, factor * values, values)


def shard_levels(own_key, extent, pieces, smallest, largest):
    level, own = 1.0, jax.random.fold_in(own_key, 6)
    for axis_at, blocks in pieces:
        draws = jnp.exp(jax.random.uniform(jax.random.fold_in(own, axis_at), (blocks,), jnp.float32, smallest / len(pieces), largest / len(pieces)))
        level = level * jnp.repeat(draws, extent[axis_at] // blocks).reshape([-1 if axis == axis_at else 1 for axis in range(len(extent))])
    return level


def scatter_about(rng, extent, scale, reach, shards=(), kind=jnp.bfloat16):
    values = scale * jax.random.normal(rng, extent, jnp.float32)
    if shards:
        values = values * shard_levels(rng, extent, shards, -0.22, 0.18)
    return jnp.clip(values, -reach, reach).astype(kind)


def noise_with(key, dims, spread, reach, shards, heavy, kind=jnp.bfloat16):
    array = spread * jax.random.normal(key, dims, jnp.float32)
    if shards:
        array = array * shard_levels(key, dims, shards, -0.22, 0.18)
    return jnp.clip(spiked(array, jax.random.fold_in(key, 3), *heavy), -reach, reach).astype(kind)


def setup_inputs(seed: int = 0, part: int = 0) -> dict:
    splits = jax.random.split(jax.random.key(seed), 8)
    part_splits = jax.random.split(jax.random.fold_in(splits[7], part), 8)
    return {
        "inputs": scatter_about(part_splits[0], (TOKS, B, D), 1.0, 6.0, ((2, 8),)),
        "gains": jnp.clip(1.0 + 0.1 * jax.random.normal(splits[1], (LAYERS, D), jnp.float32), 0.5, 1.5),
        "decays": jnp.clip(jnp.exp(math.log(0.999) - 0.35567447 * jax.random.uniform(splits[2], (LAYERS, H), jnp.float32) ** shard_levels(splits[2], (LAYERS, H), ((1, 8),), -0.2, 0.2)), 0.7, 0.999),
        "w_qkv": scatter_about(splits[3], (LAYERS, D, 3, H, HD), D ** -0.5, 0.09375, ((3, 8),)),
        "w_out": noise_with(splits[4], (LAYERS, H, HD, D), (H * HD) ** -0.5, 0.125, ((1, 8),), (1, 3, 8, 2.0)),
        "s_state": scatter_about(part_splits[5], (LAYERS, B, H, HD, HD), HD ** -0.5, 0.5, ((2, 8),), jnp.float32),
        "r_state": draw_r_state(jax.random.fold_in(jax.random.fold_in(splits[7], part), 71), part),
    }


EPSILON = 1e-05
PRECISE = lax.Precision.HIGHEST

def rescale(vector):
    return vector * lax.rsqrt(lax.optimization_barrier(jnp.mean(vector * vector, axis=-1, keepdims=True)) + EPSILON)

def mesa_step(query_vec, key_vec, value_vec, decay, states, inverse):
    applied = jnp.einsum('bhij,bhj->bhi', inverse, key_vec, precision=PRECISE)
    denominator = decay[None, :] + lax.optimization_barrier(jnp.sum(key_vec * applied, axis=-1))
    inverse = (inverse - applied[..., :, None] * applied[..., None, :] / denominator[..., None, None]) / decay[None, :, None, None]
    states = decay[None, :, None, None] * states + value_vec[..., :, None] * key_vec[..., None, :]
    weighted = jnp.einsum('bhij,bhj->bhi', inverse, query_vec, precision=PRECISE)
    output = jnp.einsum('bhij,bhj->bhi', states, weighted, precision=PRECISE)
    return (output, states, inverse)

def reference(inputs, gains, decays, w_qkv, w_out, s_state, r_state):
    stream = inputs.astype(jnp.float32)
    states = [s_state[index] for index in range(LAYERS)]
    inverses = [r_state[index] for index in range(LAYERS)]
    results = []
    for position in range(TOKS):
        current = stream[position]
        for layer_id in range(LAYERS):
            normed = (rescale(current) * gains[layer_id]).astype(jnp.bfloat16)
            projected = jnp.dot(normed, w_qkv[layer_id].reshape(D, 3 * H * HD), preferred_element_type=jnp.float32).reshape(B, 3, H, HD)
            query_vec = rescale(projected[:, 0])
            key_vec = rescale(projected[:, 1]) * HD ** (-0.5)
            value_vec = projected[:, 2]
            output, states[layer_id], inverses[layer_id] = mesa_step(query_vec, key_vec, value_vec, decays[layer_id], states[layer_id], inverses[layer_id])
            mixed = jnp.dot(output.astype(jnp.bfloat16).reshape(B, H * HD), w_out[layer_id].reshape(H * HD, D), preferred_element_type=jnp.float32)
            current = current + mixed
        results.append(current)
    return (jnp.stack(results), jnp.stack(states), jnp.stack(inverses))
```

```python
import functools

import jax
import jax.numpy as jnp
from jax import lax
from jax.experimental import pallas as pl
from jax.experimental.pallas import tpu as pltpu
from jax.sharding import PartitionSpec as P

EPSILON = 1e-05
RING = 4
CHUNK = 256
F32 = jnp.float32
BF16 = jnp.bfloat16
MESH = pl.DeviceIdType.MESH


def front_kernel(
    n, tokens, batch, heads, layers,
    x_ref, gains_ref, dec_ref, w_hbm, wo_hbm, s_hbm, r_hbm,
    y_ref, left_ref, right_ref,
    raw, wide, rep, wo, sv, rv, xg, lhs, acc, part, recv, cur, kq, pz, os, oo,
    raw_sem, in_sem, send_sem, recv_sem, own_sem,
):
    me = lax.axis_index("head")
    rows = tokens * batch
    hd = kq.shape[-1]
    width = lhs.shape[1]
    shard = x_ref.shape[1]
    mixed = 3 * heads
    chunks = width // CHUNK
    span = CHUNK * mixed

    def raw_copy(layer, c, slot):
        return pltpu.make_async_copy(
            w_hbm.at[layer, pl.ds(pl.multiple_of(c * span, span), span)],
            raw.at[slot],
            raw_sem.at[slot],
        )

    def state_copies(layer):
        return (
            pltpu.make_async_copy(r_hbm.at[layer], rv.at[layer], in_sem.at[0, layer]),
            pltpu.make_async_copy(s_hbm.at[layer], sv.at[layer], in_sem.at[1, layer]),
            pltpu.make_async_copy(wo_hbm.at[layer], wo.at[layer], in_sem.at[2, layer]),
        )

    def fill(layer):
        for c in range(min(RING, chunks)):
            raw_copy(layer, c, c).start()

    def repack(layer):
        def body(c, carry):
            slot = lax.rem(c, RING)
            raw_copy(layer, c, slot).wait()
            wide[...] = raw[slot].astype(F32)

            @pl.when(c + RING < chunks)
            def _():
                raw_copy(layer, c + RING, slot).start()

            base = pl.multiple_of(c * CHUNK, CHUNK)
            for m in range(mixed):
                rep[pl.ds(base, CHUNK), m * hd : (m + 1) * hd] = wide[
                    pl.ds(m, CHUNK, stride=mixed), :
                ].astype(BF16)
            return carry

        lax.fori_loop(0, chunks, body, 0)

    def send(src, dst, phase, peer):
        return pltpu.make_async_remote_copy(
            src_ref=src,
            dst_ref=dst,
            send_sem=send_sem.at[phase, peer],
            recv_sem=recv_sem.at[phase, me],
            device_id={"head": peer},
            device_id_type=MESH,
        )

    def peer_at(k):
        return lax.rem(me + k, n)

    def arrive(buf, phase, src):
        pltpu.make_async_copy(buf.at[src], buf.at[src], recv_sem.at[phase, src]).wait()

    fill(0)

    barrier = pltpu.get_barrier_semaphore()
    for k in range(1, n):
        pl.semaphore_signal(
            barrier, inc=1, device_id={"head": peer_at(k)}, device_id_type=MESH
        )
    pl.semaphore_wait(barrier, n - 1)

    def gather_start(layer, src):
        for k in range(1, n):
            send(src, xg.at[layer, me], 2 * layer, peer_at(k)).start()
        pltpu.make_async_copy(src, xg.at[layer, me], own_sem.at[0]).start()

    def gather_wait(layer, src):
        for k in range(1, n):
            arrive(xg.at[layer], 2 * layer, peer_at(k))
        pltpu.make_async_copy(src, xg.at[layer, me], own_sem.at[0]).wait()

    def project(layer):
        total = jnp.zeros((rows, 1), F32)
        for i in range(n):
            block = xg[layer, i].astype(F32)
            total = total + jnp.sum(block * block, axis=-1, keepdims=True)
            gain = gains_ref[layer, :, i * shard : (i + 1) * shard]
            lhs[:, i * shard : (i + 1) * shard] = (block * gain).astype(BF16)
        for at in range(0, mixed * hd, 2 * hd):
            stop = min(at + 2 * hd, mixed * hd)
            acc[:, at:stop] = jnp.dot(
                lhs[...], rep[:, at:stop], preferred_element_type=F32
            )
        return lax.rsqrt(total / width + EPSILON)

    def norm(v):
        return v * lax.rsqrt(jnp.mean(v * v, axis=-1, keepdims=True) + EPSILON)

    def dots(a, b):
        return jnp.sum(a * b, axis=-1, keepdims=True)

    def tok(t):
        return slice(t * batch, (t + 1) * batch)

    def per_pair(fn):
        step = 4 if batch % 4 == 0 else 1

        def body(i, carry):
            for j in range(step):
                b = i * step + j
                for h in range(heads):
                    fn(b, h)
            return carry

        lax.fori_loop(0, batch // step, body, 0)

    def mesa(layer, factor):
        copies = state_copies(layer)
        for h in range(heads):
            cols = [slice((j * heads + h) * hd, (j * heads + h + 1) * hd) for j in range(3)]
            kq[h, rows:, :] = norm(acc[:, cols[0]] * factor)
            kq[h, :rows, :] = norm(acc[:, cols[1]] * factor) * hd ** (-0.5)
            left_ref[layer, h, rows:, :] = acc[:, cols[2]] * factor
        copies[0].wait()

        def first(b, h):
            pair = kq[h, pl.ds(b, 2 * tokens, stride=batch), :].astype(BF16)
            pz[h, pl.ds(b, 2 * tokens, stride=batch), :] = jnp.dot(
                pair, rv[layer, b, h].astype(BF16), preferred_element_type=F32
            )

        per_pair(first)
        for h in range(heads):
            g = jnp.full((batch, 1), dec_ref[layer, h], F32)
            ginv = 1.0 / g
            ks = [kq[h, tok(t), :] for t in range(tokens)]
            qs = [kq[h, tok(tokens + t), :] for t in range(tokens)]
            ps = [pz[h, tok(t), :] for t in range(tokens)]
            zs = [pz[h, tok(tokens + t), :] for t in range(tokens)]
            back = [None] * (tokens + 1)
            front = [None] * (tokens + 1)
            back[0] = front[0] = jnp.ones_like(g)
            for t in range(tokens):
                back[t + 1] = back[t] * ginv
                front[t + 1] = front[t] * g
            for t in range(tokens):
                u = ps[t]
                inv = 1.0 / (g + dots(ks[t], u))
                for s in range(t + 1, tokens):
                    ps[s] = (ps[s] - u * (dots(u, ks[s]) * inv)) * ginv
                for s in range(t, tokens):
                    zs[s] = (zs[s] - u * (dots(u, qs[s]) * inv)) * ginv
                left_ref[layer, h, tok(t), :] = u
                right_ref[layer, h, tok(t), :] = u * (-inv * back[tokens - t])
                right_ref[layer, h, tok(tokens + t), :] = ks[t] * front[tokens - 1 - t]
                pz[h, tok(t), :] = zs[t]
        copies[1].wait()

        def second(b, h):
            pair = pz[h, pl.ds(b, 2 * tokens, stride=batch), :].astype(BF16)
            os[h, pl.ds(b, 2 * tokens, stride=batch), :] = lax.dot_general(
                pair, sv[layer, b, h].astype(BF16), (((1,), (1,)), ((), ())),
                preferred_element_type=F32,
            )

        per_pair(second)
        for h in range(heads):
            g = jnp.full((batch, 1), dec_ref[layer, h], F32)
            front = [jnp.ones_like(g)]
            for t in range(tokens):
                front.append(front[-1] * g)
            for t in range(tokens):
                w = pz[h, tok(t), :]
                out = os[h, tok(t), :] * front[t + 1]
                for s in range(t + 1):
                    v = left_ref[layer, h, tok(tokens + s), :]
                    out = out + v * (dots(kq[h, tok(s), :], w) * front[t - s])
                oo[tok(t), h * hd : (h + 1) * hd] = out.astype(BF16)
        copies[2].wait()

    def mix(layer):
        phase = 2 * layer + 1
        for k in list(range(1, n)):
            p = peer_at(k)
            col = pl.ds(pl.multiple_of(p * shard, shard), shard)
            part[layer, p] = jnp.dot(
                oo[...], wo[layer, :, col], preferred_element_type=F32
            ).astype(BF16)
            send(part.at[layer, p], recv.at[layer, me], phase, p).start()
        col = pl.ds(pl.multiple_of(me * shard, shard), shard)
        return jnp.dot(oo[...], wo[layer, :, col], preferred_element_type=F32)

    def collect(layer):
        total = cur[...]
        for k in range(1, n):
            p = peer_at(k)
            arrive(recv.at[layer], 2 * layer + 1, p)
            total = total + recv[layer, p].astype(F32)
        return total

    gather_start(0, x_ref)
    repack(0)
    for layer in range(layers):
        for copy in state_copies(layer):
            copy.start()
    if layers > 1:
        fill(1)
    cur[...] = x_ref[...].astype(F32)
    gather_wait(0, x_ref)
    for layer in range(layers):
        factor = project(layer)
        mesa(layer, factor)
        cur[...] = cur[...] + mix(layer)
        if layer + 1 < layers:
            repack(layer + 1)
            if layer + 2 < layers:
                fill(layer + 2)
            total = collect(layer)
            cur[...] = total
            xg[layer + 1, me] = total.astype(BF16)
            for k in range(1, n):
                send(
                    xg.at[layer + 1, me], xg.at[layer + 1, me], 2 * layer + 2, peer_at(k)
                ).start()
            for k in range(1, n):
                arrive(xg.at[layer + 1], 2 * layer + 2, peer_at(k))
        else:
            y_ref[...] = collect(layer)
    for layer in range(layers):
        for k in range(1, n):
            p = peer_at(k)
            send(x_ref, xg.at[layer, me], 2 * layer, p).wait_send()
            send(part.at[layer, p], recv.at[layer, me], 2 * layer + 1, p).wait_send()


def state_kernel(tokens, batch, heads, dec_ref, left_ref, right_ref, r_ref, s_ref, s_out, r_out):
    layer = pl.program_id(0)
    step = pl.program_id(1)
    count = r_ref.shape[1]
    hd = r_ref.shape[-1]
    upper = lax.broadcasted_iota(jnp.int32, (2 * tokens, hd), 0) < tokens
    for i in range(count):
        b = step * count + i
        for h in range(heads):
            g = jnp.full((1, hd), dec_ref[layer, h], F32)
            power = g
            for _ in range(tokens - 1):
                power = power * g
            rows = pl.ds(b, 2 * tokens, stride=batch)
            left = left_ref[0, h, rows, :]
            right = right_ref[0, h, rows, :]
            zero = jnp.zeros_like(right)
            both = jnp.concatenate(
                [jnp.where(upper, right, zero), jnp.where(upper, zero, right)], axis=1
            ).astype(BF16)
            update = jnp.dot(left.T.astype(BF16), both, preferred_element_type=F32)
            r_out[0, i, h] = r_ref[0, i, h] * (1.0 / power) + update[:, :hd]
            s_out[0, i, h] = s_ref[0, i, h] * power + update[:, hd:]


def on_device(n, inputs, gains, decays, w_qkv, w_out, s_state, r_state):
    layers, width, _, heads, hd = w_qkv.shape
    tokens, batch, shard = inputs.shape
    rows = tokens * batch
    mixed = 3 * heads
    vmem = pl.BlockSpec(memory_space=pltpu.VMEM)
    smem = pl.BlockSpec(memory_space=pltpu.SMEM)
    anywhere = pl.BlockSpec(memory_space=pl.ANY)
    pairs = (layers, heads, 2 * rows, hd)
    y, left, right = pl.pallas_call(
        functools.partial(front_kernel, n, tokens, batch, heads, layers),
        out_shape=(
            jax.ShapeDtypeStruct((rows, shard), F32),
            jax.ShapeDtypeStruct(pairs, F32),
            jax.ShapeDtypeStruct(pairs, F32),
        ),
        in_specs=[vmem, vmem, smem, anywhere, anywhere, anywhere, anywhere],
        out_specs=(vmem, vmem, vmem),
        scratch_shapes=[
            pltpu.VMEM((RING, CHUNK * mixed, hd), BF16),
            pltpu.VMEM((CHUNK * mixed, hd), F32),
            pltpu.VMEM((width, mixed * hd), BF16),
            pltpu.VMEM((layers, heads * hd, width), BF16),
            pltpu.VMEM((layers, batch, heads, hd, hd), F32),
            pltpu.VMEM((layers, batch, heads, hd, hd), F32),
            pltpu.VMEM((layers, n, rows, shard), BF16),
            pltpu.VMEM((rows, width), BF16),
            pltpu.VMEM((rows, mixed * hd), F32),
            pltpu.VMEM((layers, n, rows, shard), BF16),
            pltpu.VMEM((layers, n, rows, shard), BF16),
            pltpu.VMEM((rows, shard), F32),
            pltpu.VMEM((heads, 2 * rows, hd), F32),
            pltpu.VMEM((heads, 2 * rows, hd), F32),
            pltpu.VMEM((heads, 2 * rows, hd), F32),
            pltpu.VMEM((rows, heads * hd), BF16),
            pltpu.SemaphoreType.DMA((RING,)),
            pltpu.SemaphoreType.DMA((3, layers)),
            pltpu.SemaphoreType.DMA((2 * layers, n)),
            pltpu.SemaphoreType.DMA((2 * layers, n)),
            pltpu.SemaphoreType.DMA((1,)),
        ],
        compiler_params=pltpu.CompilerParams(
            collective_id=0, has_side_effects=True, vmem_limit_bytes=62 * 1024 * 1024
        ),
        name="front",
    )(
        inputs.reshape(rows, shard),
        gains.reshape(layers, 1, width),
        decays,
        w_qkv.reshape(layers, width * mixed, hd),
        w_out.reshape(layers, heads * hd, width),
        s_state,
        r_state,
    )
    count = 4 if batch % 4 == 0 else 1
    block = pl.BlockSpec((1, count, heads, hd, hd), lambda l, b: (l, b, 0, 0, 0))
    side = pl.BlockSpec((1, heads, 2 * rows, hd), lambda l, b: (l, 0, 0, 0))
    s_final, r_final = pl.pallas_call(
        functools.partial(state_kernel, tokens, batch, heads),
        grid=(layers, batch // count),
        out_shape=(
            jax.ShapeDtypeStruct(s_state.shape, F32),
            jax.ShapeDtypeStruct(r_state.shape, F32),
        ),
        in_specs=[smem, side, side, block, block],
        out_specs=(block, block),
        compiler_params=pltpu.CompilerParams(
            dimension_semantics=("arbitrary", "arbitrary")
        ),
        name="states",
    )(decays, left, right, r_state, s_state)
    return y.reshape(tokens, batch, shard), s_final, r_final


def solution(mesh):
    in_specs = (
        P(None, "grp", "head"),
        P(),
        P(None, "head"),
        P(None, None, None, "head", None),
        P(None, "head", None, None),
        P(None, "grp", "head", None, None),
        P(None, "grp", "head", None, None),
    )
    out_specs = (
        P(None, "grp", "head"),
        P(None, "grp", "head", None, None),
        P(None, "grp", "head", None, None),
    )
    return jax.shard_map(
        functools.partial(on_device, mesh.shape["head"]),
        mesh=mesh,
        in_specs=in_specs,
        out_specs=out_specs,
        check_vma=False,
    )
```

```python
import functools

import jax
import jax.numpy as jnp
from jax import lax
from jax.experimental import pallas as pl
from jax.experimental.pallas import tpu as pltpu
from jax.sharding import PartitionSpec as P

EPSILON = 1e-05
RING = 4
CHUNK = 256
F32 = jnp.float32
BF16 = jnp.bfloat16
MESH = pl.DeviceIdType.MESH


def front_kernel(
    n, tokens, batch, heads, layers,
    x_ref, gains_ref, dec_ref, w_hbm, wo_hbm, s_hbm, r_hbm,
    y_ref, sv, rv,
    left_ref, right_ref, raw, wide, rep, wo, xg, lhs, acc, part, recv, cur, kq, pz, os, oo,
    raw_sem, in_sem, send_sem, recv_sem, own_sem,
):
    me = lax.axis_index("head")
    rows = tokens * batch
    hd = kq.shape[-1]
    width = lhs.shape[1]
    shard = x_ref.shape[1]
    mixed = 3 * heads
    chunks = width // CHUNK
    span = CHUNK * mixed

    def raw_copy(layer, c, slot):
        return pltpu.make_async_copy(
            w_hbm.at[layer, pl.ds(pl.multiple_of(c * span, span), span)],
            raw.at[slot],
            raw_sem.at[slot],
        )

    def state_copies(layer):
        return (
            pltpu.make_async_copy(r_hbm.at[layer], rv.at[layer], in_sem.at[0, layer]),
            pltpu.make_async_copy(s_hbm.at[layer], sv.at[layer], in_sem.at[1, layer]),
            pltpu.make_async_copy(wo_hbm.at[layer], wo.at[layer], in_sem.at[2, layer]),
        )

    def fill(layer):
        for c in range(min(RING, chunks)):
            raw_copy(layer, c, c).start()

    def repack(layer):
        def body(c, carry):
            slot = lax.rem(c, RING)
            raw_copy(layer, c, slot).wait()
            wide[...] = raw[slot].astype(F32)

            @pl.when(c + RING < chunks)
            def _():
                raw_copy(layer, c + RING, slot).start()

            base = pl.multiple_of(c * CHUNK, CHUNK)
            for m in range(mixed):
                rep[pl.ds(base, CHUNK), m * hd : (m + 1) * hd] = wide[
                    pl.ds(m, CHUNK, stride=mixed), :
                ].astype(BF16)
            return carry

        lax.fori_loop(0, chunks, body, 0)

    def send(src, dst, phase, peer):
        return pltpu.make_async_remote_copy(
            src_ref=src,
            dst_ref=dst,
            send_sem=send_sem.at[phase, peer],
            recv_sem=recv_sem.at[phase, me],
            device_id={"head": peer},
            device_id_type=MESH,
        )

    def peer_at(k):
        return lax.rem(me + k, n)

    def arrive(buf, phase, src):
        pltpu.make_async_copy(buf.at[src], buf.at[src], recv_sem.at[phase, src]).wait()

    fill(0)

    barrier = pltpu.get_barrier_semaphore()
    for k in range(1, n):
        pl.semaphore_signal(
            barrier, inc=1, device_id={"head": peer_at(k)}, device_id_type=MESH
        )
    pl.semaphore_wait(barrier, n - 1)

    def gather_start(layer, src):
        for k in range(1, n):
            send(src, xg.at[layer, me], 2 * layer, peer_at(k)).start()
        pltpu.make_async_copy(src, xg.at[layer, me], own_sem.at[0]).start()

    def gather_wait(layer, src):
        for k in range(1, n):
            arrive(xg.at[layer], 2 * layer, peer_at(k))
        pltpu.make_async_copy(src, xg.at[layer, me], own_sem.at[0]).wait()

    def project(layer):
        total = jnp.zeros((rows, 1), F32)
        for i in range(n):
            block = xg[layer, i].astype(F32)
            total = total + jnp.sum(block * block, axis=-1, keepdims=True)
            gain = gains_ref[layer, :, i * shard : (i + 1) * shard]
            lhs[:, i * shard : (i + 1) * shard] = (block * gain).astype(BF16)
        for at in range(0, mixed * hd, 2 * hd):
            stop = min(at + 2 * hd, mixed * hd)
            acc[:, at:stop] = jnp.dot(
                lhs[...], rep[:, at:stop], preferred_element_type=F32
            )
        return lax.rsqrt(total / width + EPSILON)

    def norm(v):
        return v * lax.rsqrt(jnp.mean(v * v, axis=-1, keepdims=True) + EPSILON)

    def dots(a, b):
        return jnp.sum(a * b, axis=-1, keepdims=True)

    def tok(t):
        return slice(t * batch, (t + 1) * batch)

    def per_pair(fn):
        step = 4 if batch % 4 == 0 else 1

        def body(i, carry):
            for j in range(step):
                b = i * step + j
                for h in range(heads):
                    fn(b, h)
            return carry

        lax.fori_loop(0, batch // step, body, 0)

    def mesa(layer, factor):
        copies = state_copies(layer)
        for h in range(heads):
            cols = [slice((j * heads + h) * hd, (j * heads + h + 1) * hd) for j in range(3)]
            kq[h, rows:, :] = norm(acc[:, cols[0]] * factor)
            kq[h, :rows, :] = norm(acc[:, cols[1]] * factor) * hd ** (-0.5)
            left_ref[layer, h, rows:, :] = acc[:, cols[2]] * factor
        copies[0].wait()

        def first(b, h):
            pair = kq[h, pl.ds(b, 2 * tokens, stride=batch), :].astype(BF16)
            pz[h, pl.ds(b, 2 * tokens, stride=batch), :] = jnp.dot(
                pair, rv[layer, b, h].astype(BF16), preferred_element_type=F32
            )

        per_pair(first)
        for h in range(heads):
            g = jnp.full((batch, 1), dec_ref[layer, h], F32)
            ginv = 1.0 / g
            ks = [kq[h, tok(t), :] for t in range(tokens)]
            qs = [kq[h, tok(tokens + t), :] for t in range(tokens)]
            ps = [pz[h, tok(t), :] for t in range(tokens)]
            zs = [pz[h, tok(tokens + t), :] for t in range(tokens)]
            back = [None] * (tokens + 1)
            front = [None] * (tokens + 1)
            back[0] = front[0] = jnp.ones_like(g)
            for t in range(tokens):
                back[t + 1] = back[t] * ginv
                front[t + 1] = front[t] * g
            for t in range(tokens):
                u = ps[t]
                inv = 1.0 / (g + dots(ks[t], u))
                for s in range(t + 1, tokens):
                    ps[s] = (ps[s] - u * (dots(u, ks[s]) * inv)) * ginv
                for s in range(t, tokens):
                    zs[s] = (zs[s] - u * (dots(u, qs[s]) * inv)) * ginv
                left_ref[layer, h, tok(t), :] = u
                right_ref[layer, h, tok(t), :] = u * (-inv * back[tokens - t])
                right_ref[layer, h, tok(tokens + t), :] = ks[t] * front[tokens - 1 - t]
                pz[h, tok(t), :] = zs[t]
        copies[1].wait()

        def second(b, h):
            pair = pz[h, pl.ds(b, 2 * tokens, stride=batch), :].astype(BF16)
            os[h, pl.ds(b, 2 * tokens, stride=batch), :] = lax.dot_general(
                pair, sv[layer, b, h].astype(BF16), (((1,), (1,)), ((), ())),
                preferred_element_type=F32,
            )

        per_pair(second)
        for h in range(heads):
            g = jnp.full((batch, 1), dec_ref[layer, h], F32)
            front = [jnp.ones_like(g)]
            for t in range(tokens):
                front.append(front[-1] * g)
            for t in range(tokens):
                w = pz[h, tok(t), :]
                out = os[h, tok(t), :] * front[t + 1]
                for s in range(t + 1):
                    v = left_ref[layer, h, tok(tokens + s), :]
                    out = out + v * (dots(kq[h, tok(s), :], w) * front[t - s])
                oo[tok(t), h * hd : (h + 1) * hd] = out.astype(BF16)
        copies[2].wait()

    def update(layer):
        upper = lax.broadcasted_iota(jnp.int32, (2 * tokens, hd), 0) < tokens
        scales = []
        for h in range(heads):
            g = jnp.full((1, hd), dec_ref[layer, h], F32)
            power = g
            for _ in range(tokens - 1):
                power = power * g
            scales.append((power, 1.0 / power))

        def pair(b, h):
            near = pl.ds(b, 2 * tokens, stride=batch)
            left = left_ref[layer, h, near, :]
            right = right_ref[layer, h, near, :]
            zero = jnp.zeros_like(right)
            both = jnp.concatenate(
                [jnp.where(upper, right, zero), jnp.where(upper, zero, right)], axis=1
            ).astype(BF16)
            change = jnp.dot(left.T.astype(BF16), both, preferred_element_type=F32)
            rv[layer, b, h] = rv[layer, b, h] * scales[h][1] + change[:, :hd]
            sv[layer, b, h] = sv[layer, b, h] * scales[h][0] + change[:, hd:]

        per_pair(pair)

    def mix(layer):
        phase = 2 * layer + 1
        for k in list(range(1, n)):
            p = peer_at(k)
            col = pl.ds(pl.multiple_of(p * shard, shard), shard)
            part[layer, p] = jnp.dot(
                oo[...], wo[layer, :, col], preferred_element_type=F32
            ).astype(BF16)
            send(part.at[layer, p], recv.at[layer, me], phase, p).start()
        col = pl.ds(pl.multiple_of(me * shard, shard), shard)
        return jnp.dot(oo[...], wo[layer, :, col], preferred_element_type=F32)

    def collect(layer):
        total = cur[...]
        for k in range(1, n):
            p = peer_at(k)
            arrive(recv.at[layer], 2 * layer + 1, p)
            total = total + recv[layer, p].astype(F32)
        return total

    gather_start(0, x_ref)
    repack(0)
    for layer in range(layers):
        for copy in state_copies(layer):
            copy.start()
    if layers > 1:
        fill(1)
    cur[...] = x_ref[...].astype(F32)
    gather_wait(0, x_ref)
    for layer in range(layers):
        factor = project(layer)
        mesa(layer, factor)
        cur[...] = cur[...] + mix(layer)
        if layer + 1 < layers:
            repack(layer + 1)
            if layer + 2 < layers:
                fill(layer + 2)
            total = collect(layer)
            cur[...] = total
            xg[layer + 1, me] = total.astype(BF16)
            for k in range(1, n):
                send(
                    xg.at[layer + 1, me], xg.at[layer + 1, me], 2 * layer + 2, peer_at(k)
                ).start()
            update(layer)
            for k in range(1, n):
                arrive(xg.at[layer + 1], 2 * layer + 2, peer_at(k))
        else:
            update(layer)
            y_ref[...] = collect(layer)
    for layer in range(layers):
        for k in range(1, n):
            p = peer_at(k)
            send(x_ref, xg.at[layer, me], 2 * layer, p).wait_send()
            send(part.at[layer, p], recv.at[layer, me], 2 * layer + 1, p).wait_send()


def on_device(n, inputs, gains, decays, w_qkv, w_out, s_state, r_state):
    layers, width, _, heads, hd = w_qkv.shape
    tokens, batch, shard = inputs.shape
    rows = tokens * batch
    mixed = 3 * heads
    vmem = pl.BlockSpec(memory_space=pltpu.VMEM)
    smem = pl.BlockSpec(memory_space=pltpu.SMEM)
    anywhere = pl.BlockSpec(memory_space=pl.ANY)
    pairs = (layers, heads, 2 * rows, hd)
    y, s_new, r_new = pl.pallas_call(
        functools.partial(front_kernel, n, tokens, batch, heads, layers),
        out_shape=(
            pltpu.VMEM((rows, shard), F32),
            pltpu.VMEM(s_state.shape, F32),
            pltpu.VMEM(r_state.shape, F32),
        ),
        in_specs=[vmem, vmem, smem, anywhere, anywhere, anywhere, anywhere],
        out_specs=(vmem, vmem, vmem),
        scratch_shapes=[
            pltpu.VMEM(pairs, F32),
            pltpu.VMEM(pairs, F32),
            pltpu.VMEM((RING, CHUNK * mixed, hd), BF16),
            pltpu.VMEM((CHUNK * mixed, hd), F32),
            pltpu.VMEM((width, mixed * hd), BF16),
            pltpu.VMEM((layers, heads * hd, width), BF16),
            pltpu.VMEM((layers, n, rows, shard), BF16),
            pltpu.VMEM((rows, width), BF16),
            pltpu.VMEM((rows, mixed * hd), F32),
            pltpu.VMEM((layers, n, rows, shard), BF16),
            pltpu.VMEM((layers, n, rows, shard), BF16),
            pltpu.VMEM((rows, shard), F32),
            pltpu.VMEM((heads, 2 * rows, hd), F32),
            pltpu.VMEM((heads, 2 * rows, hd), F32),
            pltpu.VMEM((heads, 2 * rows, hd), F32),
            pltpu.VMEM((rows, heads * hd), BF16),
            pltpu.SemaphoreType.DMA((RING,)),
            pltpu.SemaphoreType.DMA((3, layers)),
            pltpu.SemaphoreType.DMA((2 * layers, n)),
            pltpu.SemaphoreType.DMA((2 * layers, n)),
            pltpu.SemaphoreType.DMA((1,)),
        ],
        compiler_params=pltpu.CompilerParams(
            collective_id=0, has_side_effects=True, vmem_limit_bytes=42 * 1024 * 1024
        ),
        name="front",
    )(
        inputs.reshape(rows, shard),
        gains.reshape(layers, 1, width),
        decays,
        w_qkv.reshape(layers, width * mixed, hd),
        w_out.reshape(layers, heads * hd, width),
        s_state,
        r_state,
    )
    return y.reshape(tokens, batch, shard), s_new, r_new


def solution(mesh):
    in_specs = (
        P(None, "grp", "head"),
        P(),
        P(None, "head"),
        P(None, None, None, "head", None),
        P(None, "head", None, None),
        P(None, "grp", "head", None, None),
        P(None, "grp", "head", None, None),
    )
    out_specs = (
        P(None, "grp", "head"),
        P(None, "grp", "head", None, None),
        P(None, "grp", "head", None, None),
    )
    return jax.shard_map(
        functools.partial(on_device, mesh.shape["head"]),
        mesh=mesh,
        in_specs=in_specs,
        out_specs=out_specs,
        check_vma=False,
    )
```
